32 devices in a mesh: sample: 8 (over z, y), space: 4 (over x, core).
Axes of the slice: x: 2, y: 2, z: 4, core: 2. Of those that a mesh axis runs over, the one named last changes fastest.
Arguments:
- features: bfloat16 [8, 64, 256, 256], P('sample', 'space'), may hold values from -6 to 6
- weight_one: bfloat16 [3, 3, 256, 256], P(None, None, None, 'sample'), may hold values from -0.125 to 0.125
- offset_one: float32 [256], replicated, may hold values from -0.5 to 0.5
- weight_two: bfloat16 [3, 3, 256, 256], P(None, None, None, 'sample'), may hold values from -0.125 to 0.125
- offset_two: float32 [256], replicated, may hold values from -0.5 to 0.5
Outputs:
- context: bfloat16 [8, 64, 256, 256], P('sample', 'space')
The draws below stay inside these ranges and needn't reach their ends.
All inputs are finite; a program needn't handle non-finite values.
Results may differ from the reference program's by a relative error of at most 0.0047.
Values may be sent and summed in bfloat16 or wider, within the bound.
A program may use at most 192 MiB of HBM per device.

```python
import jax
import jax.numpy as jnp
from jax import lax

C = 256
DILATION_RATE = 8
W = 256
H = 64
S = 8


def block_levels(own_key, shape, cuts, low, largest):
    factor_of = 1.0
    for axis_at, shards_of in cuts:
        draws = jax.random.uniform(jax.random.fold_in(jax.random.fold_in(own_key, 6), axis_at), (shards_of,), jnp.float32, low / len(cuts), largest / len(cuts))
        factor_of = factor_of * jnp.repeat(jnp.exp(draws), shape[axis_at] // shards_of).reshape((-1,) + (1,) * (len(shape) - 1 - axis_at))
    return factor_of


def centred(own_key, extent, width, limit, split=(), held_as=jnp.bfloat16):
    level = block_levels(own_key, extent, split, -0.22, 0.18) if split else 1.0
    entries = jax.random.normal(own_key, extent, jnp.float32) * width * level
    return jnp.minimum(jnp.maximum(entries, -limit), limit).astype(held_as)


def setup_inputs(seed: int = 0) -> dict:
    key_list = jax.random.split(jax.random.key(seed), 6)
    features = centred(key_list[0], (S, H, W, C), 1.0, 6.0, ((0, 8), (1, 4)))
    weight_one = centred(key_list[1], (3, 3, C, C), (9 * C) ** -0.5, 0.125, ((3, 8),))
    offset_one = jnp.clip(jax.random.uniform(key_list[2], (C,), jnp.float32, -0.5, 0.5), -0.5, 0.5)
    weight_two = centred(key_list[3], (3, 3, C, C), (9 * C) ** -0.5, 0.125, ((3, 8),))
    offset_two = jnp.clip(jax.random.uniform(key_list[4], (C,), jnp.float32, -0.5, 0.5), -0.5, 0.5)
    return {"features": features, "weight_one": weight_one, "offset_one": offset_one, "weight_two": weight_two, "offset_two": offset_two}


def conv_layer(feature_values, kernel_weights, offset):
    tap_sum = lax.conv_general_dilated(feature_values[None], kernel_weights, (1, 1), ((DILATION_RATE, DILATION_RATE), (DILATION_RATE, DILATION_RATE)), rhs_dilation=(DILATION_RATE, DILATION_RATE), dimension_numbers=("NHWC", "HWIO", "NHWC"), preferred_element_type=jnp.float32)
    return jnp.maximum(tap_sum[0] + offset, 0.0)


def reference(features, weight_one, offset_one, weight_two, offset_two):
    def one_sample(single):
        hidden = conv_layer(single, weight_one, offset_one).astype(jnp.bfloat16)
        return conv_layer(hidden, weight_two, offset_two).astype(jnp.bfloat16)
    return lax.map(one_sample, features)
```

```python
import functools

import jax
import jax.numpy as jnp
from jax import lax
from jax.experimental import pallas as pl
from jax.experimental.pallas import tpu as pltpu
from jax.sharding import PartitionSpec as P

MESH = pl.DeviceIdType.MESH
D = 8
R = 2


def kernel(
    n_sample, n_space, f_ref, w1_ref, w2_ref, b1_ref, b2_ref, out_ref,
    x, h, wloc, wt, obuf,
    loc_sem, out_sem, bar_unused,
    near_sem, far_s, far_r, hnear_s, hnear_r, hfar_s, hfar_r,
    z_s, z_r, y_s, y_r, c_s, c_r,
):
    rows, width, chans = out_ref.shape[1:]
    chunks = D // R
    n_hi = n_sample // 2
    o_loc = wloc.shape[-1]
    half = chans // 2
    space = lax.axis_index("space")
    sample = lax.axis_index("sample")
    odd = lax.rem(space, 2)
    hi, lo = sample // 2, lax.rem(sample, 2)

    near = space + 1 - 2 * odd
    far = space - 1 + 2 * odd
    has_far = jnp.logical_and(far >= 0, far < n_space)
    far_group, near_group = 1 + odd, 2 - odd
    far_halo, near_halo = 3 * D * odd, 3 * D * (1 - odd)

    feat_in = pltpu.make_async_copy(f_ref.at[0], x.at[pl.ds(D, rows)], loc_sem.at[0])
    w_in = [
        pltpu.make_async_copy(w, wloc.at[l], loc_sem.at[1 + l])
        for l, w in enumerate((w1_ref, w2_ref))
    ]
    w_in[0].start()
    w_in[1].start()
    feat_in.start()

    barrier = pltpu.get_barrier_semaphore()
    peers = [{"space": near}, {"sample": hi * 2 + 1 - lo}]
    peers += [{"sample": lax.rem(hi + k, n_hi) * 2 + lo} for k in range(1, n_hi)]
    for peer in peers:
        pl.semaphore_signal(barrier, inc=1, device_id=peer, device_id_type=MESH)

    @pl.when(has_far)
    def _():
        pl.semaphore_signal(barrier, inc=1, device_id={"space": far}, device_id_type=MESH)
        pl.semaphore_wait(barrier, len(peers) + 1)

    @pl.when(jnp.logical_not(has_far))
    def _():
        pl.semaphore_wait(barrier, len(peers))

    def remote(src, dst, send, recv, peer):
        return pltpu.make_async_remote_copy(
            src_ref=src, dst_ref=dst, send_sem=send, recv_sem=recv,
            device_id=peer, device_id_type=MESH,
        )

    def feat_far(i):
        return remote(
            f_ref.at[0, pl.ds(D * odd + R * i, R)],
            x.at[pl.ds(3 * D * (1 - odd) + R * i, R)],
            far_s.at[i], far_r.at[i], {"space": far},
        )

    def hid_far(i):
        return remote(
            h.at[pl.ds(D * far_group + R * i, R)],
            h.at[pl.ds(3 * D * (1 - odd) + R * i, R)],
            hfar_s.at[i], hfar_r.at[i], {"space": far},
        )

    feat_near = remote(
        f_ref.at[0, pl.ds(D * (1 - odd), D)],
        x.at[pl.ds(3 * D * odd, D)],
        near_sem.at[0], near_sem.at[1], {"space": near},
    )

    def hid_near(i):
        return remote(
            h.at[pl.ds(D * near_group + R * i, R)],
            h.at[pl.ds(3 * D * odd + R * i, R)],
            hnear_s.at[i], hnear_r.at[i], {"space": near},
        )

    @pl.when(has_far)
    def _():
        for i in range(chunks):
            feat_far(i).start()

    def piece(l, k, q, which):
        owner = lax.rem(hi - k + n_hi, n_hi) * 2 + (lo if q == 0 else 1 - lo)
        start = pl.multiple_of(owner * o_loc, o_loc)
        lane = pl.multiple_of(which * half, half)
        return wt.at[l, :, pl.ds(start, o_loc), pl.ds(lane, half)]

    def z_copy(l, k):
        ref = piece(l, 0, 0, odd)
        return remote(ref, ref, z_s.at[l, k], z_r.at[l, k], {"sample": lax.rem(hi + k, n_hi) * 2 + lo})

    def z_arrived(l, k):
        ref = piece(l, k, 0, odd)
        return remote(ref, ref, z_s.at[l, k], z_r.at[l, k], {"sample": lax.rem(hi + k, n_hi) * 2 + lo})

    def y_copy(l, k):
        ref = piece(l, k, 0, odd)
        return remote(ref, ref, y_s.at[l, k], y_r.at[l, k], {"sample": hi * 2 + 1 - lo})

    def y_arrived(l, k):
        ref = piece(l, k, 1, odd)
        return remote(ref, ref, y_s.at[l, k], y_r.at[l, k], {"sample": hi * 2 + 1 - lo})

    def c_copy(l, k, q):
        ref = piece(l, k, q, odd)
        return remote(ref, ref, c_s.at[l, k, q], c_r.at[l, k, q], {"space": near})

    def c_arrived(l, k, q):
        ref = piece(l, k, q, 1 - odd)
        return remote(ref, ref, c_s.at[l, k, q], c_r.at[l, k, q], {"space": near})

    def scatter(l):
        w_in[l].wait()
        start = pl.multiple_of(sample * o_loc, o_loc)
        for a in range(3):
            for b in range(3):
                wt[l, 3 * a + b, pl.ds(start, o_loc), :] = wloc[l, a, b].T
        for k in range(1, n_hi):
            z_copy(l, k).start()
        y_copy(l, 0).start()

    def forward_z(l):
        for k in range(1, n_hi):
            z_arrived(l, k).wait_recv()
            y_copy(l, k).start()
            c_copy(l, k, 0).start()

    def forward_y(l):
        for k in range(n_hi):
            y_arrived(l, k).wait_recv()
            c_copy(l, k, 1).start()

    def collect(l):
        for k in range(n_hi):
            for q in range(2):
                if (k, q) != (0, 0):
                    c_arrived(l, k, q).wait_recv()

    def sent(l):
        for k in range(n_hi):
            y_copy(l, k).wait_send()
            if k:
                z_copy(l, k).wait_send()
            for q in range(2):
                if (k, q) != (0, 0):
                    c_copy(l, k, q).wait_send()

    scatter(0)
    feat_near.start()
    scatter(1)

    @pl.when(jnp.logical_not(has_far))
    def _():
        zero = jnp.zeros((D, width, chans), jnp.bfloat16)
        x[pl.ds(far_halo, D)] = zero
        h[pl.ds(far_halo, D)] = zero

    forward_z(0)
    forward_y(0)
    feat_in.wait()
    feat_near.wait_recv()
    collect(0)

    def conv_rows(src, l, bias, group, i):
        lhs = jnp.concatenate(
            [src[pl.ds(D * (group + a - 1) + R * i, R)].reshape(R * width, chans) for a in range(3)], axis=1
        )
        ys = []
        for b in range(3):
            rhs = jnp.concatenate([wt[l, 3 * a + b] for a in range(3)], axis=1)
            y = lax.dot_general(lhs, rhs, (((1,), (1,)), ((), ())), preferred_element_type=jnp.float32)
            ys.append(y.reshape(R, width, chans))
        zero = jnp.zeros((R, D, chans), jnp.float32)
        low = jnp.concatenate([zero, ys[0][:, : width - D]], axis=1)
        high = jnp.concatenate([ys[2][:, D:], zero], axis=1)
        total = ys[1] + low + high + bias[...].reshape(1, 1, chans)
        return jnp.maximum(total, 0.0).astype(jnp.bfloat16)

    def hidden_far(i, carry):
        @pl.when(has_far)
        def _():
            feat_far(i).wait_recv()

        h[pl.ds(D * far_group + R * i, R)] = conv_rows(x, 0, b1_ref, far_group, i)

        @pl.when(has_far)
        def _():
            hid_far(i).start()

        return carry

    def hidden_near(i, carry):
        h[pl.ds(D * near_group + R * i, R)] = conv_rows(x, 0, b1_ref, near_group, i)
        hid_near(i).start()
        return carry

    def put(group, i):
        row = D * (group - 1) + R * i
        return pltpu.make_async_copy(
            obuf.at[pl.ds(row, R)], out_ref.at[0, pl.ds(row, R)], out_sem.at[group - 1, i]
        )

    def context_near(i, carry):
        hid_near(i).wait_recv()
        obuf[pl.ds(D * (near_group - 1) + R * i, R)] = conv_rows(h, 1, b2_ref, near_group, i)
        put(near_group, i).start()
        return carry

    def context_far(i, carry):
        @pl.when(has_far)
        def _():
            hid_far(i).wait_recv()

        obuf[pl.ds(D * (far_group - 1) + R * i, R)] = conv_rows(h, 1, b2_ref, far_group, i)
        put(far_group, i).start()
        return carry

    lax.fori_loop(0, chunks, hidden_far, 0)
    forward_z(1)
    lax.fori_loop(0, chunks, hidden_near, 0)
    forward_y(1)
    collect(1)
    lax.fori_loop(0, chunks, context_near, 0)
    lax.fori_loop(0, chunks, context_far, 0)

    feat_near.wait_send()
    sent(0)
    sent(1)
    for i in range(chunks):
        hid_near(i).wait_send()

    @pl.when(has_far)
    def _():
        for i in range(chunks):
            feat_far(i).wait_send()
            hid_far(i).wait_send()

    for i in range(chunks):
        put(near_group, i).wait()
        put(far_group, i).wait()


def solution(mesh):
    n_sample, n_space = mesh.shape["sample"], mesh.shape["space"]
    assert n_sample % 2 == 0 and n_space % 2 == 0

    def per_device(features, weight_one, offset_one, weight_two, offset_two):
        _, rows, width, chans = features.shape
        assert features.shape[0] == 1 and rows == 2 * D
        o_loc = weight_one.shape[-1]
        n_hi, chunks = n_sample // 2, D // R
        bf16, dma = jnp.bfloat16, pltpu.SemaphoreType.DMA
        anywhere = pl.BlockSpec(memory_space=pl.ANY)
        vmem = pl.BlockSpec(memory_space=pltpu.VMEM)
        return pl.pallas_call(
            functools.partial(kernel, n_sample, n_space),
            out_shape=jax.ShapeDtypeStruct(features.shape, bf16),
            in_specs=[anywhere, anywhere, anywhere, vmem, vmem],
            out_specs=anywhere,
            scratch_shapes=[
                pltpu.VMEM((4 * D, width, chans), bf16),
                pltpu.VMEM((4 * D, width, chans), bf16),
                pltpu.VMEM((2, 3, 3, chans, o_loc), bf16),
                pltpu.VMEM((2, 9, chans, chans), bf16),
                pltpu.VMEM((rows, width, chans), bf16),
                dma((3,)), dma((2, chunks)), dma((1,)),
                dma((2,)), dma((chunks,)), dma((chunks,)),
                dma((chunks,)), dma((chunks,)), dma((chunks,)), dma((chunks,)),
                dma((2, n_hi)), dma((2, n_hi)), dma((2, n_hi)), dma((2, n_hi)),
                dma((2, n_hi, 2)), dma((2, n_hi, 2)),
            ],
            compiler_params=pltpu.CompilerParams(
                collective_id=0, has_side_effects=True, vmem_limit_bytes=60 << 20
            ),
            name="context_module",
        )(features, weight_one, weight_two, offset_one.reshape(1, chans), offset_two.reshape(1, chans))

    return jax.shard_map(
        per_device,
        mesh=mesh,
        in_specs=(
            P("sample", "space", None, None),
            P(None, None, None, "sample"),
            P(),
            P(None, None, None, "sample"),
            P(),
        ),
        out_specs=P("sample", "space", None, None),
        check_vma=False,
    )
```

```python
import functools

import jax
import jax.numpy as jnp
from jax import lax
from jax.experimental import pallas as pl
from jax.experimental.pallas import tpu as pltpu
from jax.sharding import PartitionSpec as P

MESH = pl.DeviceIdType.MESH
D = 8
R = 2


def kernel(
    n_sample, n_space, f_ref, w1_ref, w2_ref, b1_ref, b2_ref, out_ref,
    x, h, wt, obuf, loc_sem, out_sem,
    near_sem, far_s, far_r, hnear_s, hnear_r, hfar_s, hfar_r,
    z_s, z_r, y_s, y_r, c_s, c_r,
):
    rows, width, chans = out_ref.shape[1:]
    chunks = D // R
    n_hi = n_sample // 2
    o_loc = w1_ref.shape[1]
    weights = (w1_ref, w2_ref)
    half = chans // 2
    space = lax.axis_index("space")
    sample = lax.axis_index("sample")
    odd = lax.rem(space, 2)
    hi, lo = sample // 2, lax.rem(sample, 2)

    near = space + 1 - 2 * odd
    far = space - 1 + 2 * odd
    has_far = jnp.logical_and(far >= 0, far < n_space)
    far_group, near_group = 1 + odd, 2 - odd
    far_halo, near_halo = 3 * D * odd, 3 * D * (1 - odd)

    feat_in = pltpu.make_async_copy(f_ref.at[0], x.at[pl.ds(D, rows)], loc_sem.at[0])
    own = pl.ds(pl.multiple_of(sample * o_loc, o_loc), o_loc)
    w_in = [pltpu.make_async_copy(w, wt.at[l, :, own], loc_sem.at[1 + l]) for l, w in enumerate(weights)]
    w_in[0].start()
    w_in[1].start()
    feat_in.start()

    barrier = pltpu.get_barrier_semaphore()
    peers = [{"space": near}, {"sample": hi * 2 + 1 - lo}]
    peers += [{"sample": lax.rem(hi + k, n_hi) * 2 + lo} for k in range(1, n_hi)]
    for peer in peers:
        pl.semaphore_signal(barrier, inc=1, device_id=peer, device_id_type=MESH)

    @pl.when(has_far)
    def _():
        pl.semaphore_signal(barrier, inc=1, device_id={"space": far}, device_id_type=MESH)
        pl.semaphore_wait(barrier, len(peers) + 1)

    @pl.when(jnp.logical_not(has_far))
    def _():
        pl.semaphore_wait(barrier, len(peers))

    def remote(src, dst, send, recv, peer):
        return pltpu.make_async_remote_copy(
            src_ref=src, dst_ref=dst, send_sem=send, recv_sem=recv,
            device_id=peer, device_id_type=MESH,
        )

    def feat_far(i):
        return remote(
            f_ref.at[0, pl.ds(D * odd + R * i, R)],
            x.at[pl.ds(3 * D * (1 - odd) + R * i, R)],
            far_s.at[i], far_r.at[i], {"space": far},
        )

    def hid_far(i):
        return remote(
            h.at[pl.ds(D * far_group + R * i, R)],
            h.at[pl.ds(3 * D * (1 - odd) + R * i, R)],
            hfar_s.at[i], hfar_r.at[i], {"space": far},
        )

    feat_near = remote(
        f_ref.at[0, pl.ds(D * (1 - odd), D)],
        x.at[pl.ds(3 * D * odd, D)],
        near_sem.at[0], near_sem.at[1], {"space": near},
    )

    def hid_near(i):
        return remote(
            h.at[pl.ds(D * near_group + R * i, R)],
            h.at[pl.ds(3 * D * odd + R * i, R)],
            hnear_s.at[i], hnear_r.at[i], {"space": near},
        )

    @pl.when(has_far)
    def _():
        for i in range(chunks):
            feat_far(i).start()

    def piece(l, k, q, which):
        owner = lax.rem(hi - k + n_hi, n_hi) * 2 + (lo if q == 0 else 1 - lo)
        start = pl.multiple_of(owner * o_loc, o_loc)
        lane = pl.multiple_of(which * half, half)
        return wt.at[l, :, pl.ds(start, o_loc), pl.ds(lane, half)]

    def shard(l):
        return weights[l].at[:, :, pl.ds(pl.multiple_of(odd * half, half), half)]

    def z_copy(l, k):
        return remote(shard(l), piece(l, 0, 0, odd), z_s.at[l, k], z_r.at[l, k], {"sample": lax.rem(hi + k, n_hi) * 2 + lo})

    def z_arrived(l, k):
        ref = piece(l, k, 0, odd)
        return remote(ref, ref, z_s.at[l, k], z_r.at[l, k], {"sample": lax.rem(hi + k, n_hi) * 2 + lo})

    def y_copy(l, k):
        ref = piece(l, k, 0, odd)
        return remote(ref if k else shard(l), ref, y_s.at[l, k], y_r.at[l, k], {"sample": hi * 2 + 1 - lo})

    def y_arrived(l, k):
        ref = piece(l, k, 1, odd)
        return remote(ref, ref, y_s.at[l, k], y_r.at[l, k], {"sample": hi * 2 + 1 - lo})

    def c_copy(l, k, q):
        ref = piece(l, k, q, odd)
        return remote(ref, ref, c_s.at[l, k, q], c_r.at[l, k, q], {"space": near})

    def c_arrived(l, k, q):
        ref = piece(l, k, q, 1 - odd)
        return remote(ref, ref, c_s.at[l, k, q], c_r.at[l, k, q], {"space": near})

    def scatter(l):
        for k in range(1, n_hi):
            z_copy(l, k).start()
        y_copy(l, 0).start()

    def forward_z(l):
        for k in range(1, n_hi):
            z_arrived(l, k).wait_recv()
            y_copy(l, k).start()
            c_copy(l, k, 0).start()

    def forward_y(l):
        for k in range(n_hi):
            y_arrived(l, k).wait_recv()
            c_copy(l, k, 1).start()

    def collect(l):
        w_in[l].wait()
        for k in range(n_hi):
            for q in range(2):
                if (k, q) != (0, 0):
                    c_arrived(l, k, q).wait_recv()

    def sent(l):
        for k in range(n_hi):
            y_copy(l, k).wait_send()
            if k:
                z_copy(l, k).wait_send()
            for q in range(2):
                if (k, q) != (0, 0):
                    c_copy(l, k, q).wait_send()

    scatter(0)
    feat_near.start()
    scatter(1)

    @pl.when(jnp.logical_not(has_far))
    def _():
        zero = jnp.zeros((D, width, chans), jnp.bfloat16)
        x[pl.ds(far_halo, D)] = zero
        h[pl.ds(far_halo, D)] = zero

    forward_z(0)
    forward_y(0)
    feat_in.wait()
    feat_near.wait_recv()
    collect(0)

    def conv_rows(src, l, bias, group, i):
        lhs = jnp.concatenate(
            [src[pl.ds(D * (group + a - 1) + R * i, R)].reshape(R * width, chans) for a in range(3)], axis=1
        )
        ys = []
        for b in range(3):
            rhs = jnp.concatenate([wt[l, 3 * a + b] for a in range(3)], axis=1)
            y = lax.dot_general(lhs, rhs, (((1,), (1,)), ((), ())), preferred_element_type=jnp.float32)
            ys.append(y.reshape(R, width, chans))
        zero = jnp.zeros((R, D, chans), jnp.float32)
        low = jnp.concatenate([zero, ys[0][:, : width - D]], axis=1)
        high = jnp.concatenate([ys[2][:, D:], zero], axis=1)
        total = ys[1] + low + high + bias[...].reshape(1, 1, chans)
        return jnp.maximum(total, 0.0).astype(jnp.bfloat16)

    def hidden_far(i, carry):
        @pl.when(has_far)
        def _():
            feat_far(i).wait_recv()

        h[pl.ds(D * far_group + R * i, R)] = conv_rows(x, 0, b1_ref, far_group, i)

        @pl.when(has_far)
        def _():
            hid_far(i).start()

        return carry

    def hidden_near(i, carry):
        h[pl.ds(D * near_group + R * i, R)] = conv_rows(x, 0, b1_ref, near_group, i)
        hid_near(i).start()
        return carry

    def put(group, i):
        row = D * (group - 1) + R * i
        return pltpu.make_async_copy(
            obuf.at[pl.ds(row, R)], out_ref.at[0, pl.ds(row, R)], out_sem.at[group - 1, i]
        )

    def context_near(i, carry):
        hid_near(i).wait_recv()
        obuf[pl.ds(D * (near_group - 1) + R * i, R)] = conv_rows(h, 1, b2_ref, near_group, i)
        put(near_group, i).start()
        return carry

    def context_far(i, carry):
        @pl.when(has_far)
        def _():
            hid_far(i).wait_recv()

        obuf[pl.ds(D * (far_group - 1) + R * i, R)] = conv_rows(h, 1, b2_ref, far_group, i)
        put(far_group, i).start()
        return carry

    lax.fori_loop(0, chunks, hidden_far, 0)
    forward_z(1)
    lax.fori_loop(0, chunks, hidden_near, 0)
    forward_y(1)
    collect(1)
    lax.fori_loop(0, chunks, context_near, 0)
    lax.fori_loop(0, chunks, context_far, 0)

    feat_near.wait_send()
    sent(0)
    sent(1)
    for i in range(chunks):
        hid_near(i).wait_send()

    @pl.when(has_far)
    def _():
        for i in range(chunks):
            feat_far(i).wait_send()
            hid_far(i).wait_send()

    for i in range(chunks):
        put(near_group, i).wait()
        put(far_group, i).wait()


def solution(mesh):
    n_sample, n_space = mesh.shape["sample"], mesh.shape["space"]
    assert n_sample % 2 == 0 and n_space % 2 == 0

    def per_device(features, weight_one, offset_one, weight_two, offset_two):
        _, rows, width, chans = features.shape
        assert features.shape[0] == 1 and rows == 2 * D
        o_loc = weight_one.shape[-1]
        n_hi, chunks = n_sample // 2, D // R

        def taps(weight):
            return jnp.swapaxes(weight, 2, 3).reshape(9, o_loc, chans)

        bf16, dma = jnp.bfloat16, pltpu.SemaphoreType.DMA
        anywhere = pl.BlockSpec(memory_space=pl.ANY)
        vmem = pl.BlockSpec(memory_space=pltpu.VMEM)
        return pl.pallas_call(
            functools.partial(kernel, n_sample, n_space),
            out_shape=jax.ShapeDtypeStruct(features.shape, bf16),
            in_specs=[anywhere, anywhere, anywhere, vmem, vmem],
            out_specs=anywhere,
            scratch_shapes=[
                pltpu.VMEM((4 * D, width, chans), bf16),
                pltpu.VMEM((4 * D, width, chans), bf16),
                pltpu.VMEM((2, 9, chans, chans), bf16),
                pltpu.VMEM((rows, width, chans), bf16),
                dma((3,)), dma((2, chunks)),
                dma((2,)), dma((chunks,)), dma((chunks,)),
                dma((chunks,)), dma((chunks,)), dma((chunks,)), dma((chunks,)),
                dma((2, n_hi)), dma((2, n_hi)), dma((2, n_hi)), dma((2, n_hi)),
                dma((2, n_hi, 2)), dma((2, n_hi, 2)),
            ],
            compiler_params=pltpu.CompilerParams(
                collective_id=0, has_side_effects=True, vmem_limit_bytes=60 << 20
            ),
            name="context_module",
        )(features, taps(weight_one), taps(weight_two), offset_one.reshape(1, chans), offset_two.reshape(1, chans))

    return jax.shard_map(
        per_device,
        mesh=mesh,
        in_specs=(
            P("sample", "space", None, None),
            P(None, None, None, "sample"),
            P(),
            P(None, None, None, "sample"),
            P(),
        ),
        out_specs=P("sample", "space", None, None),
        check_vma=False,
    )
```

```python
import functools

import jax
import jax.numpy as jnp
from jax import lax
from jax.experimental import pallas as pl
from jax.experimental.pallas import tpu as pltpu
from jax.sharding import PartitionSpec as P

MESH = pl.DeviceIdType.MESH
D = 8
R = 2
B = 4


def kernel(
    n_sample, n_space, f_ref, w1_ref, w2_ref, b1_ref, b2_ref, out_ref,
    x, h, wt, obuf, loc_sem, out_sem,
    near_sem, far_s, far_r, hnear_s, hnear_r, hfar_s, hfar_r,
    z_s, z_r, y_s, y_r, c_s, c_r,
):
    rows, width, chans = out_ref.shape[1:]
    chunks = D // R
    n_hi = n_sample // 2
    o_loc = w1_ref.shape[1]
    weights = (w1_ref, w2_ref)
    half = chans // 2
    space = lax.axis_index("space")
    sample = lax.axis_index("sample")
    odd = lax.rem(space, 2)
    hi, lo = sample // 2, lax.rem(sample, 2)

    near = space + 1 - 2 * odd
    far = space - 1 + 2 * odd
    has_far = jnp.logical_and(far >= 0, far < n_space)
    far_group, near_group = 1 + odd, 2 - odd
    far_halo, near_halo = 3 * D * odd, 3 * D * (1 - odd)

    feat_in = pltpu.make_async_copy(f_ref.at[0], x.at[pl.ds(D, rows)], loc_sem.at[0])
    own = pl.ds(pl.multiple_of(sample * o_loc, o_loc), o_loc)
    w_in = [pltpu.make_async_copy(w, wt.at[l, :, own], loc_sem.at[1 + l]) for l, w in enumerate(weights)]
    w_in[0].start()
    w_in[1].start()
    feat_in.start()

    barrier = pltpu.get_barrier_semaphore()
    peers = [{"space": near}, {"sample": hi * 2 + 1 - lo}]
    peers += [{"sample": lax.rem(hi + k, n_hi) * 2 + lo} for k in range(1, n_hi)]
    for peer in peers:
        pl.semaphore_signal(barrier, inc=1, device_id=peer, device_id_type=MESH)

    @pl.when(has_far)
    def _():
        pl.semaphore_signal(barrier, inc=1, device_id={"space": far}, device_id_type=MESH)
        pl.semaphore_wait(barrier, len(peers) + 1)

    @pl.when(jnp.logical_not(has_far))
    def _():
        pl.semaphore_wait(barrier, len(peers))

    def remote(src, dst, send, recv, peer):
        return pltpu.make_async_remote_copy(
            src_ref=src, dst_ref=dst, send_sem=send, recv_sem=recv,
            device_id=peer, device_id_type=MESH,
        )

    def feat_far(i):
        return remote(
            f_ref.at[0, pl.ds(D * odd + R * i, R)],
            x.at[pl.ds(3 * D * (1 - odd) + R * i, R)],
            far_s.at[i], far_r.at[i], {"space": far},
        )

    def hid_far(i):
        return remote(
            h.at[pl.ds(D * far_group + R * i, R)],
            h.at[pl.ds(3 * D * (1 - odd) + R * i, R)],
            hfar_s.at[i], hfar_r.at[i], {"space": far},
        )

    feat_near = remote(
        f_ref.at[0, pl.ds(D * (1 - odd), D)],
        x.at[pl.ds(3 * D * odd, D)],
        near_sem.at[0], near_sem.at[1], {"space": near},
    )

    def hid_near(i):
        return remote(
            h.at[pl.ds(D * near_group + B * i, B)],
            h.at[pl.ds(3 * D * odd + B * i, B)],
            hnear_s.at[i], hnear_r.at[i], {"space": near},
        )

    @pl.when(has_far)
    def _():
        for i in range(chunks):
            feat_far(i).start()

    def piece(l, k, q, which):
        owner = lax.rem(hi - k + n_hi, n_hi) * 2 + (lo if q == 0 else 1 - lo)
        start = pl.multiple_of(owner * o_loc, o_loc)
        lane = pl.multiple_of(which * half, half)
        return wt.at[l, :, pl.ds(start, o_loc), pl.ds(lane, half)]

    def shard(l):
        return weights[l].at[:, :, pl.ds(pl.multiple_of(odd * half, half), half)]

    def z_copy(l, k):
        return remote(shard(l), piece(l, 0, 0, odd), z_s.at[l, k], z_r.at[l, k], {"sample": lax.rem(hi + k, n_hi) * 2 + lo})

    def z_arrived(l, k):
        ref = piece(l, k, 0, odd)
        return remote(ref, ref, z_s.at[l, k], z_r.at[l, k], {"sample": lax.rem(hi + k, n_hi) * 2 + lo})

    def y_copy(l, k):
        ref = piece(l, k, 0, odd)
        return remote(shard(l) if isinstance(k, int) and k == 0 else ref, ref, y_s.at[l, k], y_r.at[l, k], {"sample": hi * 2 + 1 - lo})

    def y_arrived(l, k):
        ref = piece(l, k, 1, odd)
        return remote(ref, ref, y_s.at[l, k], y_r.at[l, k], {"sample": hi * 2 + 1 - lo})

    def c_copy(l, k, q):
        ref = piece(l, k, q, odd)
        return remote(ref, ref, c_s.at[l, k, q], c_r.at[l, k, q], {"space": near})

    def c_arrived(l, k, q):
        ref = piece(l, k, q, 1 - odd)
        return remote(ref, ref, c_s.at[l, k, q], c_r.at[l, k, q], {"space": near})

    def scatter(l):
        for k in range(1, n_hi):
            z_copy(l, k).start()
        y_copy(l, 0).start()

    def forward_z(l, k):
        z_arrived(l, k).wait_recv()
        y_copy(l, k).start()
        c_copy(l, k, 0).start()

    def forward_y(l, k):
        y_arrived(l, k).wait_recv()
        c_copy(l, k, 1).start()

    def collect(l):
        w_in[l].wait()
        for k in range(n_hi):
            for q in range(2):
                if (k, q) != (0, 0):
                    c_arrived(l, k, q).wait_recv()

    def sent(l):
        for k in range(n_hi):
            y_copy(l, k).wait_send()
            if k:
                z_copy(l, k).wait_send()
            for q in range(2):
                if (k, q) != (0, 0):
                    c_copy(l, k, q).wait_send()

    scatter(0)
    feat_near.start()

    @pl.when(jnp.logical_not(has_far))
    def _():
        zero = jnp.zeros((D, width, chans), jnp.bfloat16)
        x[pl.ds(far_halo, D)] = zero
        h[pl.ds(far_halo, D)] = zero

    for k in range(1, n_hi):
        forward_z(0, k)
    scatter(1)
    for k in range(n_hi):
        forward_y(0, k)
    feat_in.wait()
    feat_near.wait_recv()
    collect(0)

    def conv_rows(src, l, bias, group, row, R):
        lhs = jnp.concatenate(
            [src[pl.ds(D * (group + a - 1) + row, R)].reshape(R * width, chans) for a in range(3)], axis=1
        )
        ys = []
        for b in range(3):
            rhs = jnp.concatenate([wt[l, 3 * a + b] for a in range(3)], axis=1)
            y = lax.dot_general(lhs, rhs, (((1,), (1,)), ((), ())), preferred_element_type=jnp.float32)
            ys.append(y.reshape(R, width, chans))
        zero = jnp.zeros((R, D, chans), jnp.float32)
        low = jnp.concatenate([zero, ys[0][:, : width - D]], axis=1)
        high = jnp.concatenate([ys[2][:, D:], zero], axis=1)
        total = ys[1] + low + high + bias[...].reshape(1, 1, chans)
        return jnp.maximum(total, 0.0).astype(jnp.bfloat16)

    def hidden_far(i, carry):
        @pl.when(has_far)
        def _():
            feat_far(i).wait_recv()

        h[pl.ds(D * far_group + R * i, R)] = conv_rows(x, 0, b1_ref, far_group, R * i, R)

        @pl.when(has_far)
        def _():
            hid_far(i).start()

        per = n_hi // chunks
        for j in range(per):

            @pl.when(i * per + j > 0)
            def _():
                forward_z(1, i * per + j)

        return carry

    def hidden_near(i, carry):
        h[pl.ds(D * near_group + B * i, B)] = conv_rows(x, 0, b1_ref, near_group, B * i, B)
        hid_near(i).start()
        per = n_hi // (D // B)
        for j in range(per):
            forward_y(1, i * per + j)
        return carry

    def put(group, i, R):
        row = D * (group - 1) + R * i
        return pltpu.make_async_copy(
            obuf.at[pl.ds(row, R)], out_ref.at[0, pl.ds(row, R)], out_sem.at[group - 1, i]
        )

    def context_near(i, carry):
        hid_near(i).wait_recv()
        obuf[pl.ds(D * (near_group - 1) + B * i, B)] = conv_rows(h, 1, b2_ref, near_group, B * i, B)
        put(near_group, i, B).start()
        return carry

    def context_far(i, carry):
        @pl.when(has_far)
        def _():
            hid_far(i).wait_recv()

        obuf[pl.ds(D * (far_group - 1) + R * i, R)] = conv_rows(h, 1, b2_ref, far_group, R * i, R)
        put(far_group, i, R).start()
        return carry

    lax.fori_loop(0, chunks, hidden_far, 0)
    lax.fori_loop(0, D // B, hidden_near, 0)
    collect(1)
    lax.fori_loop(0, D // B, context_near, 0)
    lax.fori_loop(0, chunks, context_far, 0)

    feat_near.wait_send()
    sent(0)
    sent(1)
    for i in range(D // B):
        hid_near(i).wait_send()

    @pl.when(has_far)
    def _():
        for i in range(chunks):
            feat_far(i).wait_send()
            hid_far(i).wait_send()

    for i in range(D // B):
        put(near_group, i, B).wait()
    for i in range(chunks):
        put(far_group, i, R).wait()


def solution(mesh):
    n_sample, n_space = mesh.shape["sample"], mesh.shape["space"]
    assert n_sample % 2 == 0 and n_space % 2 == 0

    def per_device(features, weight_one, offset_one, weight_two, offset_two):
        _, rows, width, chans = features.shape
        assert features.shape[0] == 1 and rows == 2 * D
        o_loc = weight_one.shape[-1]
        n_hi, chunks = n_sample // 2, D // R

        def taps(weight):
            return jnp.swapaxes(weight, 2, 3).reshape(9, o_loc, chans)

        bf16, dma = jnp.bfloat16, pltpu.SemaphoreType.DMA
        anywhere = pl.BlockSpec(memory_space=pl.ANY)
        vmem = pl.BlockSpec(memory_space=pltpu.VMEM)
        return pl.pallas_call(
            functools.partial(kernel, n_sample, n_space),
            out_shape=jax.ShapeDtypeStruct(features.shape, bf16),
            in_specs=[anywhere, anywhere, anywhere, vmem, vmem],
            out_specs=anywhere,
            scratch_shapes=[
                pltpu.VMEM((4 * D, width, chans), bf16),
                pltpu.VMEM((4 * D, width, chans), bf16),
                pltpu.VMEM((2, 9, chans, chans), bf16),
                pltpu.VMEM((rows, width, chans), bf16),
                dma((3,)), dma((2, chunks)),
                dma((2,)), dma((chunks,)), dma((chunks,)),
                dma((chunks,)), dma((chunks,)), dma((chunks,)), dma((chunks,)),
                dma((2, n_hi)), dma((2, n_hi)), dma((2, n_hi)), dma((2, n_hi)),
                dma((2, n_hi, 2)), dma((2, n_hi, 2)),
            ],
            compiler_params=pltpu.CompilerParams(
                collective_id=0, has_side_effects=True, vmem_limit_bytes=60 << 20
            ),
            name="context_module",
        )(features, taps(weight_one), taps(weight_two), offset_one.reshape(1, chans), offset_two.reshape(1, chans))

    return jax.shard_map(
        per_device,
        mesh=mesh,
        in_specs=(
            P("sample", "space", None, None),
            P(None, None, None, "sample"),
            P(),
            P(None, None, None, "sample"),
            P(),
        ),
        out_specs=P("sample", "space", None, None),
        check_vma=False,
    )
```

```python
import functools

import jax
import jax.numpy as jnp
from jax import lax
from jax.experimental import pallas as pl
from jax.experimental.pallas import tpu as pltpu
from jax.sharding import PartitionSpec as P

MESH = pl.DeviceIdType.MESH
D = 8
R = 2
B = 4


def kernel(
    n_sample, n_space, f_ref, w1_ref, w2_ref, b1_ref, b2_ref, obuf,
    x, h, wt, loc_sem,
    near_sem, far_s, far_r, hnear_s, hnear_r, hfar_s, hfar_r,
    z_s, z_r, y_s, y_r, c_s, c_r,
):
    rows, width, chans = obuf.shape
    chunks = D // R
    n_hi = n_sample // 2
    o_loc = w1_ref.shape[1]
    weights = (w1_ref, w2_ref)
    half = chans // 2
    space = lax.axis_index("space")
    sample = lax.axis_index("sample")
    odd = lax.rem(space, 2)
    hi, lo = sample // 2, lax.rem(sample, 2)

    near = space + 1 - 2 * odd
    far = space - 1 + 2 * odd
    has_far = jnp.logical_and(far >= 0, far < n_space)
    far_group, near_group = 1 + odd, 2 - odd
    far_halo, near_halo = 3 * D * odd, 3 * D * (1 - odd)

    feat_in = pltpu.make_async_copy(f_ref.at[0], x.at[pl.ds(D, rows)], loc_sem.at[0])
    own = pl.ds(pl.multiple_of(sample * o_loc, o_loc), o_loc)
    w_in = [pltpu.make_async_copy(w, wt.at[l, :, own], loc_sem.at[1 + l]) for l, w in enumerate(weights)]
    w_in[0].start()
    w_in[1].start()
    feat_in.start()

    barrier = pltpu.get_barrier_semaphore()
    peers = [{"space": near}, {"sample": hi * 2 + 1 - lo}]
    peers += [{"sample": lax.rem(hi + k, n_hi) * 2 + lo} for k in range(1, n_hi)]
    for peer in peers:
        pl.semaphore_signal(barrier, inc=1, device_id=peer, device_id_type=MESH)

    @pl.when(has_far)
    def _():
        pl.semaphore_signal(barrier, inc=1, device_id={"space": far}, device_id_type=MESH)
        pl.semaphore_wait(barrier, len(peers) + 1)

    @pl.when(jnp.logical_not(has_far))
    def _():
        pl.semaphore_wait(barrier, len(peers))

    def remote(src, dst, send, recv, peer):
        return pltpu.make_async_remote_copy(
            src_ref=src, dst_ref=dst, send_sem=send, recv_sem=recv,
            device_id=peer, device_id_type=MESH,
        )

    def feat_far(i):
        return remote(
            f_ref.at[0, pl.ds(D * odd + R * i, R)],
            x.at[pl.ds(3 * D * (1 - odd) + R * i, R)],
            far_s.at[i], far_r.at[i], {"space": far},
        )

    def hid_far(i):
        return remote(
            h.at[pl.ds(D * far_group + R * i, R)],
            h.at[pl.ds(3 * D * (1 - odd) + R * i, R)],
            hfar_s.at[i], hfar_r.at[i], {"space": far},
        )

    feat_near = remote(
        f_ref.at[0, pl.ds(D * (1 - odd), D)],
        x.at[pl.ds(3 * D * odd, D)],
        near_sem.at[0], near_sem.at[1], {"space": near},
    )

    def hid_near(i):
        return remote(
            h.at[pl.ds(D * near_group + B * i, B)],
            h.at[pl.ds(3 * D * odd + B * i, B)],
            hnear_s.at[i], hnear_r.at[i], {"space": near},
        )

    @pl.when(has_far)
    def _():
        for i in range(chunks):
            feat_far(i).start()

    def piece(l, k, q, which):
        owner = lax.rem(hi - k + n_hi, n_hi) * 2 + (lo if q == 0 else 1 - lo)
        start = pl.multiple_of(owner * o_loc, o_loc)
        lane = pl.multiple_of(which * half, half)
        return wt.at[l, :, pl.ds(start, o_loc), pl.ds(lane, half)]

    def shard(l):
        return weights[l].at[:, :, pl.ds(pl.multiple_of(odd * half, half), half)]

    def z_copy(l, k):
        return remote(shard(l), piece(l, 0, 0, odd), z_s.at[l, k], z_r.at[l, k], {"sample": lax.rem(hi + k, n_hi) * 2 + lo})

    def z_arrived(l, k):
        ref = piece(l, k, 0, odd)
        return remote(ref, ref, z_s.at[l, k], z_r.at[l, k], {"sample": lax.rem(hi + k, n_hi) * 2 + lo})

    def y_copy(l, k):
        ref = piece(l, k, 0, odd)
        return remote(shard(l) if isinstance(k, int) and k == 0 else ref, ref, y_s.at[l, k], y_r.at[l, k], {"sample": hi * 2 + 1 - lo})

    def y_arrived(l, k):
        ref = piece(l, k, 1, odd)
        return remote(ref, ref, y_s.at[l, k], y_r.at[l, k], {"sample": hi * 2 + 1 - lo})

    def c_copy(l, k, q):
        ref = piece(l, k, q, odd)
        return remote(ref, ref, c_s.at[l, k, q], c_r.at[l, k, q], {"space": near})

    def c_arrived(l, k, q):
        ref = piece(l, k, q, 1 - odd)
        return remote(ref, ref, c_s.at[l, k, q], c_r.at[l, k, q], {"space": near})

    def scatter(l):
        for k in range(1, n_hi):
            z_copy(l, k).start()
        y_copy(l, 0).start()

    def forward_z(l, k):
        z_arrived(l, k).wait_recv()
        y_copy(l, k).start()
        c_copy(l, k, 0).start()

    def forward_y(l, k):
        y_arrived(l, k).wait_recv()
        c_copy(l, k, 1).start()

    def collect(l):
        w_in[l].wait()
        for k in range(n_hi):
            for q in range(2):
                if (k, q) != (0, 0):
                    c_arrived(l, k, q).wait_recv()

    def sent(l):
        for k in range(n_hi):
            y_copy(l, k).wait_send()
            if k:
                z_copy(l, k).wait_send()
            for q in range(2):
                if (k, q) != (0, 0):
                    c_copy(l, k, q).wait_send()

    scatter(0)
    feat_near.start()

    @pl.when(jnp.logical_not(has_far))
    def _():
        zero = jnp.zeros((D, width, chans), jnp.bfloat16)
        x[pl.ds(far_halo, D)] = zero
        h[pl.ds(far_halo, D)] = zero

    for k in range(1, n_hi):
        forward_z(0, k)
    scatter(1)
    for k in range(n_hi):
        forward_y(0, k)
    feat_in.wait()
    feat_near.wait_recv()
    collect(0)

    def conv_rows(src, l, bias, group, row, R):
        lhs = jnp.concatenate(
            [src[pl.ds(D * (group + a - 1) + row, R)].reshape(R * width, chans) for a in range(3)], axis=1
        )
        ys = []
        for b in range(3):
            rhs = jnp.concatenate([wt[l, 3 * a + b] for a in range(3)], axis=1)
            y = lax.dot_general(lhs, rhs, (((1,), (1,)), ((), ())), preferred_element_type=jnp.float32)
            ys.append(y.reshape(R, width, chans))
        zero = jnp.zeros((R, D, chans), jnp.float32)
        low = jnp.concatenate([zero, ys[0][:, : width - D]], axis=1)
        high = jnp.concatenate([ys[2][:, D:], zero], axis=1)
        total = ys[1] + low + high + bias[...].reshape(1, 1, chans)
        return jnp.maximum(total, 0.0).astype(jnp.bfloat16)

    def hidden_far(i, carry):
        @pl.when(has_far)
        def _():
            feat_far(i).wait_recv()

        h[pl.ds(D * far_group + R * i, R)] = conv_rows(x, 0, b1_ref, far_group, R * i, R)

        @pl.when(has_far)
        def _():
            hid_far(i).start()

        per = n_hi // chunks
        for j in range(per):

            @pl.when(i * per + j > 0)
            def _():
                forward_z(1, i * per + j)

        return carry

    def hidden_near(i, carry):
        h[pl.ds(D * near_group + B * i, B)] = conv_rows(x, 0, b1_ref, near_group, B * i, B)
        hid_near(i).start()
        per = n_hi // (D // B)
        for j in range(per):
            forward_y(1, i * per + j)
        return carry

    def put(group, i, R):
        row = D * (group - 1) + R * i
        return pltpu.make_async_copy(
            obuf.at[pl.ds(row, R)], out_ref.at[0, pl.ds(row, R)], out_sem.at[group - 1, i]
        )

    def context_near(i, carry):
        hid_near(i).wait_recv()
        obuf[pl.ds(D * (near_group - 1) + B * i, B)] = conv_rows(h, 1, b2_ref, near_group, B * i, B)
        return carry

    def context_far(i, carry):
        @pl.when(has_far)
        def _():
            hid_far(i).wait_recv()

        obuf[pl.ds(D * (far_group - 1) + R * i, R)] = conv_rows(h, 1, b2_ref, far_group, R * i, R)
        return carry

    lax.fori_loop(0, chunks, hidden_far, 0)
    lax.fori_loop(0, D // B, hidden_near, 0)
    collect(1)
    lax.fori_loop(0, D // B, context_near, 0)
    lax.fori_loop(0, chunks, context_far, 0)

    feat_near.wait_send()
    sent(0)
    sent(1)
    for i in range(D // B):
        hid_near(i).wait_send()

    @pl.when(has_far)
    def _():
        for i in range(chunks):
            feat_far(i).wait_send()
            hid_far(i).wait_send()


def solution(mesh):
    n_sample, n_space = mesh.shape["sample"], mesh.shape["space"]
    assert n_sample % 2 == 0 and n_space % 2 == 0

    def per_device(features, weight_one, offset_one, weight_two, offset_two):
        _, rows, width, chans = features.shape
        assert features.shape[0] == 1 and rows == 2 * D
        o_loc = weight_one.shape[-1]
        n_hi, chunks = n_sample // 2, D // R

        def taps(weight):
            return jnp.swapaxes(weight, 2, 3).reshape(9, o_loc, chans)

        bf16, dma = jnp.bfloat16, pltpu.SemaphoreType.DMA
        anywhere = pl.BlockSpec(memory_space=pl.ANY)
        vmem = pl.BlockSpec(memory_space=pltpu.VMEM)
        result = pl.pallas_call(
            functools.partial(kernel, n_sample, n_space),
            out_shape=pltpu.VMEM(features.shape[1:], bf16),
            in_specs=[anywhere, anywhere, anywhere, vmem, vmem],
            out_specs=vmem,
            scratch_shapes=[
                pltpu.VMEM((4 * D, width, chans), bf16),
                pltpu.VMEM((4 * D, width, chans), bf16),
                pltpu.VMEM((2, 9, chans, chans), bf16),
                dma((3,)),
                dma((2,)), dma((chunks,)), dma((chunks,)),
                dma((chunks,)), dma((chunks,)), dma((chunks,)), dma((chunks,)),
                dma((2, n_hi)), dma((2, n_hi)), dma((2, n_hi)), dma((2, n_hi)),
                dma((2, n_hi, 2)), dma((2, n_hi, 2)),
            ],
            compiler_params=pltpu.CompilerParams(
                collective_id=0, has_side_effects=True, vmem_limit_bytes=60 << 20
            ),
            name="context_module",
        )(features, taps(weight_one), taps(weight_two), offset_one.reshape(1, chans), offset_two.reshape(1, chans))

        def store(r_ref, o_ref, sem):
            copy = pltpu.make_async_copy(r_ref, o_ref.at[0], sem)
            copy.start()
            copy.wait()

        return pl.pallas_call(
            store,
            out_shape=jax.ShapeDtypeStruct(features.shape, bf16),
            in_specs=[vmem],
            out_specs=anywhere,
            scratch_shapes=[dma],
            name="store_context",
        )(pltpu.with_memory_space_constraint(result, pltpu.VMEM))

    return jax.shard_map(
        per_device,
        mesh=mesh,
        in_specs=(
            P("sample", "space", None, None),
            P(None, None, None, "sample"),
            P(),
            P(None, None, None, "sample"),
            P(),
        ),
        out_specs=P("sample", "space", None, None),
        check_vma=False,
    )
```

```python
import functools

import jax
import jax.numpy as jnp
from jax import lax
from jax.experimental import pallas as pl
from jax.experimental.pallas import tpu as pltpu
from jax.sharding import PartitionSpec as P

MESH = pl.DeviceIdType.MESH
D = 8
R = 2
B = 4


def kernel(
    n_sample, n_space, f_ref, w1_ref, w2_ref, b1_ref, b2_ref, obuf,
    x, h, wt, loc_sem,
    near_sem, far_s, far_r, hnear_s, hnear_r, hfar_s, hfar_r,
    z_s, z_r, y_s, y_r, c_s, c_r,
):
    rows, width, chans = obuf.shape
    chunks = D // R
    n_hi = n_sample // 2
    o_loc = w1_ref.shape[1]
    weights = (w1_ref, w2_ref)
    half = chans // 2
    space = lax.axis_index("space")
    sample = lax.axis_index("sample")
    odd = lax.rem(space, 2)
    hi, lo = sample // 2, lax.rem(sample, 2)

    near = space + 1 - 2 * odd
    far = space - 1 + 2 * odd
    has_far = jnp.logical_and(far >= 0, far < n_space)
    far_group, near_group = 1 + odd, 2 - odd
    far_halo, near_halo = 3 * D * odd, 3 * D * (1 - odd)

    feat_in = pltpu.make_async_copy(f_ref.at[0], x.at[pl.ds(D, rows)], loc_sem.at[0])
    own = pl.ds(pl.multiple_of(sample * o_loc, o_loc), o_loc)
    w_in = [pltpu.make_async_copy(w, wt.at[l, :, own], loc_sem.at[1 + l]) for l, w in enumerate(weights)]
    w_in[0].start()
    w_in[1].start()
    feat_in.start()

    barrier = pltpu.get_barrier_semaphore()
    peers = [{"space": near}, {"sample": hi * 2 + 1 - lo}]
    peers += [{"sample": lax.rem(hi + k, n_hi) * 2 + lo} for k in range(1, n_hi)]
    for peer in peers:
        pl.semaphore_signal(barrier, inc=1, device_id=peer, device_id_type=MESH)

    @pl.when(has_far)
    def _():
        pl.semaphore_signal(barrier, inc=1, device_id={"space": far}, device_id_type=MESH)
        pl.semaphore_wait(barrier, len(peers) + 1)

    @pl.when(jnp.logical_not(has_far))
    def _():
        pl.semaphore_wait(barrier, len(peers))

    def remote(src, dst, send, recv, peer):
        return pltpu.make_async_remote_copy(
            src_ref=src, dst_ref=dst, send_sem=send, recv_sem=recv,
            device_id=peer, device_id_type=MESH,
        )

    def feat_far(i):
        return remote(
            f_ref.at[0, pl.ds(D * odd + R * i, R)],
            x.at[pl.ds(3 * D * (1 - odd) + R * i, R)],
            far_s.at[i], far_r.at[i], {"space": far},
        )

    def hid_far(i):
        return remote(
            h.at[pl.ds(D * far_group + R * i, R)],
            h.at[pl.ds(3 * D * (1 - odd) + R * i, R)],
            hfar_s.at[i], hfar_r.at[i], {"space": far},
        )

    feat_near = remote(
        f_ref.at[0, pl.ds(D * (1 - odd), D)],
        x.at[pl.ds(3 * D * odd, D)],
        near_sem.at[0], near_sem.at[1], {"space": near},
    )

    def hid_near(i):
        return remote(
            h.at[pl.ds(D * near_group + B * i, B)],
            h.at[pl.ds(3 * D * odd + B * i, B)],
            hnear_s.at[i], hnear_r.at[i], {"space": near},
        )

    @pl.when(has_far)
    def _():
        for i in range(chunks):
            feat_far(i).start()

    def piece(l, k, q, which):
        owner = lax.rem(hi - k + n_hi, n_hi) * 2 + (lo if q == 0 else 1 - lo)
        start = pl.multiple_of(owner * o_loc, o_loc)
        lane = pl.multiple_of(which * half, half)
        return wt.at[l, :, pl.ds(start, o_loc), pl.ds(lane, half)]

    def shard(l):
        return weights[l].at[:, :, pl.ds(pl.multiple_of(odd * half, half), half)]

    def z_copy(l, k):
        return remote(shard(l), piece(l, 0, 0, odd), z_s.at[l, k], z_r.at[l, k], {"sample": lax.rem(hi + k, n_hi) * 2 + lo})

    def z_arrived(l, k):
        ref = piece(l, k, 0, odd)
        return remote(ref, ref, z_s.at[l, k], z_r.at[l, k], {"sample": lax.rem(hi + k, n_hi) * 2 + lo})

    def y_copy(l, k):
        ref = piece(l, k, 0, odd)
        return remote(shard(l) if isinstance(k, int) and k == 0 else ref, ref, y_s.at[l, k], y_r.at[l, k], {"sample": hi * 2 + 1 - lo})

    def y_arrived(l, k):
        ref = piece(l, k, 1, odd)
        return remote(ref, ref, y_s.at[l, k], y_r.at[l, k], {"sample": hi * 2 + 1 - lo})

    def c_copy(l, k, q):
        ref = piece(l, k, q, odd)
        return remote(ref, ref, c_s.at[l, k, q], c_r.at[l, k, q], {"space": near})

    def c_arrived(l, k, q):
        ref = piece(l, k, q, 1 - odd)
        return remote(ref, ref, c_s.at[l, k, q], c_r.at[l, k, q], {"space": near})

    def scatter(l):
        for k in range(1, n_hi):
            z_copy(l, k).start()

    def forward_z(l, k):
        z_arrived(l, k).wait_recv()
        y_copy(l, k).start()
        c_copy(l, k, 0).start()

    def forward_y(l, k):
        y_arrived(l, k).wait_recv()
        c_copy(l, k, 1).start()

    def collect(l):
        w_in[l].wait()
        for k in range(n_hi):
            for q in range(2):
                if (k, q) != (0, 0):
                    c_arrived(l, k, q).wait_recv()

    def sent(l):
        for k in range(n_hi):
            y_copy(l, k).wait_send()
            if k:
                z_copy(l, k).wait_send()
            for q in range(2):
                if (k, q) != (0, 0):
                    c_copy(l, k, q).wait_send()

    scatter(0)
    y_copy(0, 0).start()
    feat_near.start()

    @pl.when(jnp.logical_not(has_far))
    def _():
        zero = jnp.zeros((D, width, chans), jnp.bfloat16)
        x[pl.ds(far_halo, D)] = zero
        h[pl.ds(far_halo, D)] = zero

    for k in range(1, n_hi):
        forward_z(0, k)
        if k == n_hi // 2:
            scatter(1)
    y_copy(1, 0).start()
    for k in range(n_hi):
        forward_y(0, k)
    feat_in.wait()
    feat_near.wait_recv()
    collect(0)

    def conv_rows(src, l, bias, group, row, R):
        lhs = jnp.concatenate(
            [src[pl.ds(D * (group + a - 1) + row, R)].reshape(R * width, chans) for a in range(3)], axis=1
        )
        ys = []
        for b in range(3):
            rhs = jnp.concatenate([wt[l, 3 * a + b] for a in range(3)], axis=1)
            y = lax.dot_general(lhs, rhs, (((1,), (1,)), ((), ())), preferred_element_type=jnp.float32)
            ys.append(y.reshape(R, width, chans))
        zero = jnp.zeros((R, D, chans), jnp.float32)
        low = jnp.concatenate([zero, ys[0][:, : width - D]], axis=1)
        high = jnp.concatenate([ys[2][:, D:], zero], axis=1)
        total = ys[1] + low + high + bias[...].reshape(1, 1, chans)
        return jnp.maximum(total, 0.0).astype(jnp.bfloat16)

    def hidden_far(i, carry):
        @pl.when(has_far)
        def _():
            feat_far(i).wait_recv()

        h[pl.ds(D * far_group + R * i, R)] = conv_rows(x, 0, b1_ref, far_group, R * i, R)

        @pl.when(has_far)
        def _():
            hid_far(i).start()

        per = n_hi // chunks
        for j in range(per):

            @pl.when(i * per + j > 0)
            def _():
                forward_z(1, i * per + j)

        return carry

    def hidden_near(i, carry):
        h[pl.ds(D * near_group + B * i, B)] = conv_rows(x, 0, b1_ref, near_group, B * i, B)
        hid_near(i).start()
        per = n_hi // (D // B)
        for j in range(per):
            forward_y(1, i * per + j)
        return carry

    def put(group, i, R):
        row = D * (group - 1) + R * i
        return pltpu.make_async_copy(
            obuf.at[pl.ds(row, R)], out_ref.at[0, pl.ds(row, R)], out_sem.at[group - 1, i]
        )

    def context_near(i, carry):
        hid_near(i).wait_recv()
        obuf[pl.ds(D * (near_group - 1) + B * i, B)] = conv_rows(h, 1, b2_ref, near_group, B * i, B)
        return carry

    def context_far(i, size):
        @pl.when(has_far)
        def _():
            for j in range(size // R):
                hid_far(i + j).wait_recv()

        obuf[pl.ds(D * (far_group - 1) + R * i, size)] = conv_rows(h, 1, b2_ref, far_group, R * i, size)

    def context_far_end(i, carry):
        context_far(i, R)
        return carry

    lax.fori_loop(0, chunks, hidden_far, 0)
    lax.fori_loop(0, D // B, hidden_near, 0)
    collect(1)
    lax.fori_loop(0, D // B, context_near, 0)
    context_far(0, B)
    lax.fori_loop(B // R, chunks, context_far_end, 0)

    feat_near.wait_send()
    sent(0)
    sent(1)
    for i in range(D // B):
        hid_near(i).wait_send()

    @pl.when(has_far)
    def _():
        for i in range(chunks):
            feat_far(i).wait_send()
            hid_far(i).wait_send()


def solution(mesh):
    n_sample, n_space = mesh.shape["sample"], mesh.shape["space"]
    assert n_sample % 2 == 0 and n_space % 2 == 0

    def per_device(features, weight_one, offset_one, weight_two, offset_two):
        _, rows, width, chans = features.shape
        assert features.shape[0] == 1 and rows == 2 * D
        o_loc = weight_one.shape[-1]
        n_hi, chunks = n_sample // 2, D // R

        def taps(weight):
            return jnp.swapaxes(weight, 2, 3).reshape(9, o_loc, chans)

        bf16, dma = jnp.bfloat16, pltpu.SemaphoreType.DMA
        anywhere = pl.BlockSpec(memory_space=pl.ANY)
        vmem = pl.BlockSpec(memory_space=pltpu.VMEM)
        result = pl.pallas_call(
            functools.partial(kernel, n_sample, n_space),
            out_shape=pltpu.VMEM(features.shape[1:], bf16),
            in_specs=[anywhere, anywhere, anywhere, vmem, vmem],
            out_specs=vmem,
            scratch_shapes=[
                pltpu.VMEM((4 * D, width, chans), bf16),
                pltpu.VMEM((4 * D, width, chans), bf16),
                pltpu.VMEM((2, 9, chans, chans), bf16),
                dma((3,)),
                dma((2,)), dma((chunks,)), dma((chunks,)),
                dma((chunks,)), dma((chunks,)), dma((chunks,)), dma((chunks,)),
                dma((2, n_hi)), dma((2, n_hi)), dma((2, n_hi)), dma((2, n_hi)),
                dma((2, n_hi, 2)), dma((2, n_hi, 2)),
            ],
            compiler_params=pltpu.CompilerParams(
                collective_id=0, has_side_effects=True, vmem_limit_bytes=60 << 20
            ),
            name="context_module",
        )(features, taps(weight_one), taps(weight_two), offset_one.reshape(1, chans), offset_two.reshape(1, chans))

        def store(r_ref, o_ref, sem):
            copy = pltpu.make_async_copy(r_ref, o_ref.at[0], sem)
            copy.start()
            copy.wait()

        return pl.pallas_call(
            store,
            out_shape=jax.ShapeDtypeStruct(features.shape, bf16),
            in_specs=[vmem],
            out_specs=anywhere,
            scratch_shapes=[dma],
            name="store_context",
        )(pltpu.with_memory_space_constraint(result, pltpu.VMEM))

    return jax.shard_map(
        per_device,
        mesh=mesh,
        in_specs=(
            P("sample", "space", None, None),
            P(None, None, None, "sample"),
            P(),
            P(None, None, None, "sample"),
            P(),
        ),
        out_specs=P("sample", "space", None, None),
        check_vma=False,
    )
```
